256 devices in a mesh: grp: 8 (over x, core), wide: 32 (over y, z).
Axes of the slice: x: 4, y: 4, z: 8, core: 2. Of those that a mesh axis runs over, the one named last changes fastest.
Arguments:
- block_coords: int32 [6144, 3], P(('grp', 'wide')), may hold values from 0 to 511, as said below
- block_values: bfloat16 [6144, 64, 4096], P(('grp', 'wide')), may hold values from -384 to 384
- factor_b: bfloat16 [16384, 256], P('wide'), may hold values from -0.15625 to 0.15625
- factor_c: bfloat16 [16384, 256], P('wide'), may hold values from -0.15625 to 0.15625
Outputs:
- new_a: float32 [32768, 256], P(('grp', 'wide'))
The draws below stay inside these ranges and needn't reach their ends.
Inputs may be any that keep to these rules, and one draw needn't show every extreme that they name: `block_coords`: block n lies on device n // 24 of the grp-major order. On each device: every mode-1 block-row b has (b // 2) modulo the wide size equal to the device's wide index; at most 6 of its blocks have a mode-1 block-row owned by one grp index, at most 2 have a mode-2 block-row in one wide index's shard of 8 block-rows, and at most 2 likewise for mode 3; each of the three bounds is reached on every device.
All inputs are finite; a program needn't handle non-finite values.
Results may differ from the reference program's by a relative error of at most 0.00055.
Values may be sent and summed in bfloat16 or wider, within the bound.
A program may use at most 128 MiB of HBM per device.

```python
import math
import jax
import jax.numpy as jnp
from jax import lax

BS = 64
R = 256
NB_DEV = 24
RB_DEV = 8
RI_DEV = 2
CAP = 2
CAPG = 6
NBT = 6144
N1 = 32768
N_GRP = 8
N_WIDE = 32


def owner_lists(key, peer_count, capacity, device_count):
    key_first, key_rest, key_order = jax.random.split(key, 3)
    first_owner = jax.random.randint(key_first, (device_count, 1), 0, peer_count, dtype=jnp.int32)
    ticket_keys = jax.random.split(key_rest, device_count)
    tickets = jax.vmap(lambda one_key: jax.random.permutation(one_key, (peer_count - 1) * capacity))(ticket_keys)
    tickets = tickets.astype(jnp.int32)
    others = (first_owner + 1 + tickets[:, :NB_DEV - capacity] // capacity) % peer_count
    owners = jnp.concatenate([jnp.broadcast_to(first_owner, (device_count, capacity)), others], axis=1)
    order_keys = jax.random.split(key_order, device_count)
    orders = jax.vmap(lambda one_key: jax.random.permutation(one_key, NB_DEV))(order_keys).astype(jnp.int32)
    return jnp.take_along_axis(owners, orders, axis=1).astype(jnp.int32)


def draw_block_coords(key, part):
    device_count = N_GRP * N_WIDE
    wide_index = (jnp.arange(device_count, dtype=jnp.int32) % N_WIDE)[:, None]
    target_group = owner_lists(jax.random.fold_in(key, 1), N_GRP, CAPG, device_count)
    local_first = jax.random.randint(jax.random.fold_in(key, 2), (device_count, NB_DEV), 0, RI_DEV, dtype=jnp.int32)
    first_rows = (target_group * N_WIDE + wide_index) * RI_DEV + local_first
    owner_second = owner_lists(jax.random.fold_in(key, 3), N_WIDE, CAP, device_count)
    local_second = jax.random.randint(jax.random.fold_in(key, 4), (device_count, NB_DEV), 0, RB_DEV, dtype=jnp.int32)
    owner_third = owner_lists(jax.random.fold_in(key, 5), N_WIDE, CAP, device_count)
    local_third = jax.random.randint(jax.random.fold_in(key, 6), (device_count, NB_DEV), 0, RB_DEV, dtype=jnp.int32)
    second_rows = owner_second * RB_DEV + local_second
    third_rows = owner_third * RB_DEV + local_third
    stacked = jnp.stack([first_rows, second_rows, third_rows], axis=-1)
    return stacked.reshape(device_count * NB_DEV, 3).astype(jnp.int32)


def factor_draw(key):
    row_total = RB_DEV * N_WIDE * BS
    key_noise, key_common, key_load, key_scale = jax.random.split(key, 4)
    noise = jax.random.truncated_normal(key_noise, -4.0, 4.0, (row_total, R), jnp.float32)
    common = jax.random.truncated_normal(key_common, -4.0, 4.0, (row_total, 1), jnp.float32)
    loading = jax.random.uniform(key_load, (1, R), jnp.float32, 0.6, 1.4)
    column_scale = jnp.exp(jax.random.uniform(key_scale, (1, R), jnp.float32, math.log(0.5), math.log(2.0)))
    return (noise + loading * common) * column_scale / math.sqrt(row_total)


def draw_factor_b(key, part):
    return factor_draw(jax.random.fold_in(key, 11)).astype(jnp.bfloat16)


def draw_factor_c(key, part):
    return factor_draw(jax.random.fold_in(key, 12)).astype(jnp.bfloat16)


def level_of(stream_key, extent, shards, smallest, top_value):
    def one(position, parts):
        draws = jax.random.uniform(jax.random.fold_in(jax.random.fold_in(stream_key, 6), position), (parts,), jnp.float32, smallest / len(shards), top_value / len(shards))
        return jnp.repeat(jnp.exp(draws), extent[position] // parts).reshape((-1,) + (1,) * (len(extent) - position - 1))

    factor_of = one(*shards[0])
    for cut in shards[1:]:
        factor_of = factor_of * one(*cut)
    return factor_of


def gaussian(key, extent, deviation, reach, shards=(), held_as=jnp.bfloat16):
    drawn = jax.random.normal(key, extent, jnp.float32) * deviation
    if len(shards) > 0:
        drawn = level_of(key, extent, shards, -0.22, 0.18) * drawn
    return jnp.clip(drawn, min=-reach, max=reach).astype(held_as)


def setup_inputs(seed: int = 0) -> dict:
    arg_keys = jax.random.split(jax.random.key(seed), 5)
    block_coords = draw_block_coords(jax.random.fold_in(arg_keys[4], 71), 0)
    block_values = gaussian(arg_keys[1], (NBT, BS, BS * BS), (RB_DEV * N_WIDE / 4), 384.0, ((0, 256),))
    factor_b = draw_factor_b(jax.random.fold_in(arg_keys[4], 71), 0)
    factor_c = draw_factor_c(jax.random.fold_in(arg_keys[4], 71), 0)
    return dict(block_coords=block_coords, block_values=block_values, factor_b=factor_b, factor_c=factor_c)


def reference(block_coords, block_values, factor_b, factor_c):

    def add_block(summed_rows, block_item):
        coord_row, value_block = block_item
        b_rows = lax.dynamic_slice_in_dim(factor_b, (coord_row[1] * BS).astype(jnp.int32), BS, 0)
        c_rows = lax.dynamic_slice_in_dim(factor_c, (coord_row[2] * BS).astype(jnp.int32), BS, 0)
        product = lax.dot_general(value_block.astype(jnp.float32), b_rows.astype(jnp.float32), (((0,), (0,)), ((), ())), preferred_element_type=jnp.float32)
        partial_rows = jnp.sum(product.reshape(BS, BS, R) * c_rows.astype(jnp.float32)[None], axis=1)
        return (summed_rows.at[coord_row[0]].add(partial_rows), None)
    start_rows = jnp.zeros((N1 // BS, BS, R), jnp.float32)
    mttkrp, unused_out = lax.scan(add_block, start_rows, (block_coords, block_values))
    gram_b = lax.dot_general(factor_b.astype(jnp.float32), factor_b.astype(jnp.float32), (((0,), (0,)), ((), ())), preferred_element_type=jnp.float32)
    gram_c = lax.dot_general(factor_c.astype(jnp.float32), factor_c.astype(jnp.float32), (((0,), (0,)), ((), ())), preferred_element_type=jnp.float32)
    normal_matrix = gram_b * gram_c
    chol_lower = jnp.linalg.cholesky(normal_matrix)
    solved = jax.scipy.linalg.cho_solve((chol_lower, True), mttkrp.reshape(N1, R).T)
    return solved.T
```

```python
import functools, heapq
import jax, jax.numpy as jnp
from jax import lax
from jax.experimental import pallas as pl
from jax.experimental.pallas import tpu as pltpu
from jax.sharding import PartitionSpec as P

MESH = pl.DeviceIdType.MESH
BS, R = 64, 256
SHARD = 512
Q = 48
Z_AT, Z_ROWS = 4 * Q, 160
Y_AT, Y_ROWS = 4 * Q + 160, 160


def plan():
    msgs = []

    def add(name, dim, sign, src, dst, rows, deps, nbytes):
        landed = ("x", rows[1] + sign) + rows[2:] if dim == "x" else rows
        msgs.append(dict(name=name, dim=dim, sign=sign, src=src, dst=dst, rows=rows, landed=landed, deps=deps, bytes=nbytes))
        return len(msgs) - 1

    def half(sign, at, rows):
        first = (rows // 2 + 15) // 16 * 16
        return (at, first) if sign > 0 else (at + first, rows - first)

    def z_ring(tag, rows_of, pys, first_deps, count):
        ids = {}
        for d in (1, 2, 3, 4):
            for s in (1, -1):
                src = 3 + s * (d - 1)
                dst = 3 + s * d if d < 4 else 7
                rows = rows_of(None) if d < 4 else rows_of(s)
                deps = [ids[d - 1, s]] if d > 1 else list(first_deps)
                ids[d, s] = add((tag, d, s), "z", s, (pys, (src, 1)), (pys, (dst, 1)), rows, deps, count * rows[-1] * 512)
        return ids

    def at_pz(ids, pz):
        dz = pz - 3
        if dz == 0:
            return []
        return [ids[4, 1], ids[4, -1]] if dz == 4 else [ids[abs(dz), 1 if dz > 0 else -1]]

    def y_ring(tag, rows_of, pz, deps, count):
        ids = {}
        for t in (1, -1):
            rows = rows_of(None)
            ids[1, t] = add((tag, 1, t), "y", t, ((1, 1), pz), ((1 + t, 1), pz), rows, list(deps), count * rows[-1] * 512)
        for t in (1, -1):
            rows = rows_of(t)
            ids[2, t] = add((tag, 2, t), "y", t, ((1 + t, 1), pz), ((3, 1), pz), rows, [ids[1, t]], count * rows[-1] * 512)
        return ids

    def x_rows(dx, sign):
        return ("x", dx) + ((0, Q) if sign is None else half(sign, 0, Q))

    def fixed(at, rows):
        return lambda sign: ("r",) + ((at, rows) if sign is None else half(sign, at, rows))

    xz = z_ring("xz", lambda s: x_rows(0, s), (1, 1), [], 1)
    zz = z_ring("zz", fixed(Z_AT, Z_ROWS), (1, 1), [], 1)
    yy = y_ring("yy", fixed(Y_AT, Y_ROWS), (3, 1), [], 1)
    xy = y_ring("xy", lambda s: x_rows(0, s), (0, 8), list(xz.values()), 8)
    x_groups = [
        (1, (2, 3), [xz[1, 1], xz[1, -1]]),
        (1, (0, 2), [xz[2, -1], xz[3, -1]]),
        (1, (5, 3), [xz[2, 1], xz[3, 1], xz[4, 1], xz[4, -1]]),
        (2, (0, 8), [xy[1, 1]]), (0, (0, 8), [xy[1, -1]]), (3, (0, 8), [xy[2, 1], xy[2, -1]])]
    for py, pz, deps in x_groups:
        place = ((py, 1), pz)
        first = {}
        for u in (1, -1):
            rows = x_rows(0, None)
            first[u] = add(("xx", py, pz, 1, u), "x", u, place, place, rows, list(deps), pz[1] * Q * 512)
        for u in (1, -1):
            rows = x_rows(u, u)
            add(("xx", py, pz, 2, u), "x", u, place, place, rows, [first[u]], pz[1] * rows[-1] * 512)
    for pz in (3, 4, 2, 5, 1, 6, 0, 7):
        y_ring(("zy", pz), fixed(Z_AT, Z_ROWS), (pz, 1), at_pz(zz, pz), 1)
    z_ring("yzA", fixed(Y_AT, Y_ROWS), (0, 2), [yy[1, -1]], 2)
    z_ring("yzB", fixed(Y_AT, Y_ROWS), (2, 2), [yy[1, 1], yy[2, 1], yy[2, -1]], 2)
    late = {("zz", 2): [xz[2, 1], xz[2, -1]], ("zz", 3): [xz[3, 1], xz[3, -1]], ("yzA", 1): [xz[4, 1], xz[4, -1]],
            ("yzB", 1): [xz[4, 1], xz[4, -1]]}
    for m in msgs:
        m["deps"] += late.get(m["name"][:2], [])
        if m["name"][0] in (("zy", 5), ("zy", 1)) and m["name"][1] == 1:
            m["deps"] += list(xz.values())
    return msgs


def order(msgs, rate=45e3, latency=1.5):
    free = {}
    got = set()
    started = set()
    heap = []
    t_end = {}

    def issue(now):
        for i, m in enumerate(msgs):
            if i not in started and all(d in got for d in m["deps"]):
                started.add(i)
                link = (m["dim"], m["sign"])
                begin = max(now, free.get(link, 0.0))
                free[link] = begin + m["bytes"] / rate
                heapq.heappush(heap, (free[link] + latency, i))

    issue(0.0)
    seq = []
    while heap:
        t, i = heapq.heappop(heap)
        got.add(i)
        seq.append(i)
        t_end[i] = t
        issue(t)
    return seq, t_end, free


def kernel(msgs, seq, gram, b_hbm, c_hbm, full, nm, mine, g, gsib, own_sem, send, recv, sib_send, sib_recv, loc, gs, gr):
    grp, wide = lax.axis_index("grp"), lax.axis_index("wide")
    x, core = grp // 2, grp % 2
    y, z = wide // 8, wide % 8
    sib = (grp + 1 - 2 * core, wide)

    def dev(dim, s):
        if dim == "x":
            return (((x + s + 4) % 4) * 2 + core, wide)
        if dim == "y":
            return (grp, ((y + s + 4) % 4) * 8 + z)
        return (grp, y * 8 + (z + s + 8) % 8)

    def row_slice(rows):
        if rows[0] == "r":
            return pl.ds(rows[1], rows[2])
        at = ((x - rows[1] + 4) % 4) * Q + rows[2]
        return pl.ds(pl.multiple_of(at, 16), rows[3])

    def region(ref, place, rows):
        (py, npy), (pz, npz) = place
        return ref.at[pl.ds(py, npy), pl.ds(pz, npz), row_slice(rows), :]

    peers = [dev(d, s) for d in "xyz" for s in (1, -1)] + [sib]
    bar = pltpu.get_barrier_semaphore()
    for p in peers:
        pl.semaphore_signal(bar, inc=1, device_id=p, device_id_type=MESH)

    own_rows = [("x", 0, 0, Q), ("r", Z_AT, SHARD - Z_AT)]
    own_place = ((1, 1), (3, 1))
    for k, src in enumerate((b_hbm, c_hbm)):
        @pl.when(core == k)
        def _():
            for j, rows in enumerate(own_rows):
                pltpu.make_async_copy(src.at[row_slice(rows), :], mine.at[1, 3, row_slice(rows), :], own_sem.at[j]).start()
    for j, rows in enumerate(own_rows):
        pltpu.make_async_copy(b_hbm.at[row_slice(rows), :], mine.at[1, 3, row_slice(rows), :], own_sem.at[j]).wait()
    pl.semaphore_wait(bar, len(peers))

    def copy(i):
        m = msgs[i]
        return pltpu.make_async_remote_copy(
            src_ref=region(mine, m["src"], m["rows"]),
            dst_ref=region(mine, m["dst"], m["rows"]),
            send_sem=send.at[i], recv_sem=recv.at[i], device_id=dev(m["dim"], m["sign"]), device_id_type=MESH)

    def publish(place, rows):
        pltpu.make_async_remote_copy(
            src_ref=region(mine, place, rows), dst_ref=region(full.at[core], place, rows),
            send_sem=sib_send, recv_sem=sib_recv, device_id=sib, device_id_type=MESH).start()
        pltpu.make_async_copy(region(mine, place, rows), region(full.at[core], place, rows), loc).start()

    def add_gram(place, rows):
        if not gram:
            return
        (py, npy), (pz, npz) = place
        f = mine[pl.ds(py, npy), pl.ds(pz, npz), row_slice(rows), :]
        f = f.reshape(-1, R)
        g[...] += lax.dot_general(f, f, (((0,), (0,)), ((), ())), preferred_element_type=jnp.float32)

    started, got = set(), set()

    def issue():
        for i, m in enumerate(msgs):
            if i not in started and all(d in got for d in m["deps"]):
                started.add(i)
                copy(i).start()

    g[...] = jnp.zeros_like(g)
    issue()
    for rows in own_rows:
        publish(own_place, rows)
        add_gram(own_place, rows)
    for i in seq:
        copy(i).wait_recv()
        got.add(i)
        issue()
        publish(msgs[i]["dst"], msgs[i]["landed"])
        add_gram(msgs[i]["dst"], msgs[i]["landed"])
    swap = pltpu.make_async_remote_copy(src_ref=g, dst_ref=gsib, send_sem=gs, recv_sem=gr, device_id=sib, device_id_type=MESH)
    swap.start()
    for i in range(len(msgs)):
        copy(i).wait_send()
    swap.wait()
    nm[...] = g[...] * gsib[...]
    whole = pltpu.make_async_remote_copy(src_ref=mine, dst_ref=full.at[1 - core], send_sem=sib_send, recv_sem=sib_recv, device_id=sib, device_id_type=MESH)
    whole.wait()
    pltpu.make_async_copy(mine, full.at[core], loc).wait()


def gather(b, c, gram=True):
    msgs = plan()
    seq, _, _ = order(msgs)
    n = len(msgs)
    return pl.pallas_call(
        functools.partial(kernel, msgs, seq, gram),
        out_shape=(jax.ShapeDtypeStruct((2, 4, 8, SHARD, R), jnp.bfloat16), jax.ShapeDtypeStruct((R, R), jnp.float32)),
        in_specs=[pl.BlockSpec(memory_space=pl.ANY)] * 2,
        out_specs=(pl.BlockSpec(memory_space=pl.ANY), pl.BlockSpec(memory_space=pltpu.VMEM)),
        scratch_shapes=[
            pltpu.VMEM((4, 8, SHARD, R), jnp.bfloat16), pltpu.VMEM((R, R), jnp.float32), pltpu.VMEM((R, R), jnp.float32),
            pltpu.SemaphoreType.DMA((2,)), pltpu.SemaphoreType.DMA((n,)), pltpu.SemaphoreType.DMA((n,)),
            pltpu.SemaphoreType.DMA, pltpu.SemaphoreType.DMA, pltpu.SemaphoreType.DMA,
            pltpu.SemaphoreType.DMA, pltpu.SemaphoreType.DMA],
        compiler_params=pltpu.CompilerParams(collective_id=0, has_side_effects=True, vmem_limit_bytes=48 << 20),
        name="gather_factors",
    )(b, c)


NB = 64
HI = lax.Precision.HIGHEST


def sweep(m_ref, k, nb=NB):
    n = m_ref.shape[0]
    at = k * nb
    panel = m_ref[at:at + nb, :]
    r = panel
    lane = lax.broadcasted_iota(jnp.int32, (1, n), 1)
    row = lax.broadcasted_iota(jnp.int32, (nb, 1), 0)
    for j in range(nb):
        col = panel[:, at + j:at + j + 1]
        pivot = panel[j:j + 1, :]
        inv = 1.0 / col[j:j + 1, :]
        scaled = jnp.where(lane == at + j, inv, pivot * inv)
        cleared = jnp.where(lane == at + j, 0.0, panel)
        panel = jnp.where(row == j, scaled, cleared - col * scaled)
    inside = (lane >= at) & (lane < at + nb)
    w = jnp.where(inside, -panel, panel)
    m = m_ref[...]
    upd = lax.dot_general(r, w, (((0,), (0,)), ((), ())), precision=HI, preferred_element_type=jnp.float32)
    m_ref[...] = jnp.where(inside, 0.0, m) - upd
    m_ref[at:at + nb, :] = w


def block_body(chunk, where, v_ref, b_ref, c_ref, acc_ref):
    n = pl.program_id(0)

    @pl.when(n == 0)
    def _():
        acc_ref[...] = jnp.zeros_like(acc_ref)

    slot = where[n, 0]
    b = b_ref[0, 0, 0]
    c = c_ref[0, 0, 0].astype(jnp.float32)
    per = chunk // BS
    for q in range(BS // per):
        prod = lax.dot_general(v_ref[0, :, q * chunk:(q + 1) * chunk], b, (((0,), (0,)), ((), ())),
                               preferred_element_type=jnp.float32)
        acc_ref[slot, q * per:(q + 1) * per, :] += jnp.sum(prod.reshape(per, BS, R) * c[None], axis=1)


def block_sums(where, values, full):
    count = values.shape[0]

    def rows(m, col):
        return lambda n, s: (m, s[n, col], s[n, col + 1], s[n, col + 2], 0)

    grid_spec = pltpu.PrefetchScalarGridSpec(
        num_scalar_prefetch=1, grid=(count,),
        in_specs=[pl.BlockSpec((1, BS, BS * BS), lambda n, s: (n, 0, 0)),
                  pl.BlockSpec((1, 1, 1, BS, R), rows(0, 1)),
                  pl.BlockSpec((1, 1, 1, BS, R), rows(1, 4))],
        out_specs=pl.BlockSpec((16, BS, R), lambda n, s: (0, 0, 0)))
    return pl.pallas_call(
        functools.partial(block_body, 512), out_shape=jax.ShapeDtypeStruct((16, BS, R), jnp.float32),
        grid_spec=grid_spec, compiler_params=pltpu.CompilerParams(vmem_limit_bytes=40 << 20), name="block_sums",
    )(where, values, full, full)


def owner_body(acc, nm, out, m, pair, mine, parts, s1, r1, s2, r2):
    grp, wide = lax.axis_index("grp"), lax.axis_index("wide")
    x, core = grp // 2, grp % 2
    sib = (grp + 1 - 2 * core, wide)
    far = [(((x + d) % 4) * 2 + core, wide) for d in (1, 2, 3)]
    bar = pltpu.get_barrier_semaphore()
    for p in far + [sib]:
        pl.semaphore_signal(bar, inc=1, device_id=p, device_id_type=MESH)
    pl.semaphore_wait(bar, 4)
    swap = pltpu.make_async_remote_copy(src_ref=acc.at[:, 1 - core], dst_ref=pair, send_sem=s1, recv_sem=r1,
                                        device_id=sib, device_id_type=MESH)
    swap.start()
    m[...] = nm[...]
    blocks = R // NB
    sweep(m, 0)
    swap.wait()
    mine[...] = acc[:, core] + pair[...]
    copies = []
    for d in (2, 1, 3):
        copies.append(pltpu.make_async_remote_copy(
            src_ref=mine.at[(x + d) % 4], dst_ref=parts.at[d - 1], send_sem=s2.at[d - 1], recv_sem=r2.at[d - 1],
            device_id=far[d - 1], device_id_type=MESH))
        copies[-1].start()
    for k in range(1, blocks):
        sweep(m, k)
    for copy in copies:
        copy.wait()
    rows = mine[x] + parts[0] + parts[1] + parts[2]
    out[...] = -jnp.dot(rows, m[...], precision=HI, preferred_element_type=jnp.float32)


def owner_rows(acc, nm):
    rows = 2 * BS
    vmem = pl.BlockSpec(memory_space=pltpu.VMEM)
    return pl.pallas_call(
        owner_body, out_shape=jax.ShapeDtypeStruct((rows, R), jnp.float32), in_specs=[vmem, vmem], out_specs=vmem,
        scratch_shapes=[
            pltpu.VMEM((R, R), jnp.float32), pltpu.VMEM((4, rows, R), jnp.float32), pltpu.VMEM((4, rows, R), jnp.float32),
            pltpu.VMEM((3, rows, R), jnp.float32), pltpu.SemaphoreType.DMA, pltpu.SemaphoreType.DMA,
            pltpu.SemaphoreType.DMA((3,)), pltpu.SemaphoreType.DMA((3,))],
        compiler_params=pltpu.CompilerParams(collective_id=1, has_side_effects=True, vmem_limit_bytes=32 << 20),
        name="owner_rows",
    )(acc.reshape(4, 2, rows, R), nm)


def local(block_coords, block_values, factor_b, factor_c):
    wide = lax.axis_index("wide")
    y, z = wide // 8, wide % 8
    first, second, third = block_coords[:, 0], block_coords[:, 1], block_coords[:, 2]

    def place(rows):
        owner = rows // 8
        return [(y - owner // 8 + 1) % 4, (z - owner % 8 + 3) % 8, rows % 8]

    where = jnp.stack([first // 64 * 2 + first % 2] + place(second) + place(third), axis=1)
    full, nm = gather(factor_b, factor_c)
    acc = block_sums(where, block_values, full)
    return owner_rows(acc, nm)


def solution(mesh):
    in_specs = (P(("grp", "wide"), None), P(("grp", "wide"), None, None), P("wide", None), P("wide", None))
    return jax.shard_map(local, mesh=mesh, in_specs=in_specs, out_specs=P(("grp", "wide"), None), check_vma=False)
```

```python
import functools
import heapq

import jax
import jax.numpy as jnp
from jax import lax
from jax.experimental import pallas as pl
from jax.experimental.pallas import tpu as pltpu
from jax.sharding import PartitionSpec as P

MESH = pl.DeviceIdType.MESH
HI = lax.Precision.HIGHEST
BS, R = 64, 256
NB, GROUP, LANES = 64, 8, 128
SHARD, G = 512, 16
Q = 48
Z_AT, Z_ROWS = 4 * Q, 176
Y_AT, Y_ROWS = 4 * Q + 176, 144


RANK = (
    60, 25, 53, 36, 4, 44, 5, 89, 1, 51, 76, 24, 46, 9, 2, 95, 61, 74, 78, 49, 6, 7,
    91, 81, 32, 12, 33, 52, 27, 57, 31, 19, 88, 39, 58, 56, 73, 64, 10, 66, 72, 20, 85, 16,
    67, 41, 38, 93, 83, 47, 0, 18, 42, 82, 34, 90, 94, 22, 84, 70, 23, 29, 86, 26, 80, 59,
    17, 40, 63, 71, 28, 14, 54, 50, 79, 92, 43, 62, 3, 21, 55, 45, 30, 37, 13, 87, 69, 11,
    8, 75, 48, 77, 15, 35, 65, 68)
HOLD = (
    (2, 1), (10, 24), (11, 6), (15, 25), (18, 53), (24, 2), (27, 51), (28, 48), (30, 28), (33, 4),
    (34, 10), (35, 27), (37, 30), (39, 11), (42, 77), (43, 88), (47, 75), (50, 60), (55, 56), (57, 20),
    (58, 75), (59, 35), (61, 1), (62, 19), (63, 50), (64, 52), (66, 53), (67, 23), (68, 60), (69, 30),
    (70, 32), (71, 35), (72, 70), (73, 17), (74, 60), (77, 73), (78, 20), (79, 84), (82, 89), (84, 88),
    (85, 37), (86, 82), (88, 0), (89, 56), (90, 27), (91, 10), (92, 81), (93, 73), (95, 38))


def plan():
    msgs = []

    def add(name, dim, sign, src, dst, rows, deps, nbytes):
        landed = ("x", rows[1] + sign) + rows[2:] if dim == "x" else rows
        msgs.append(dict(name=name, dim=dim, sign=sign, src=src, dst=dst, rows=rows, landed=landed, deps=deps, bytes=nbytes))
        return len(msgs) - 1

    def half(sign, at, rows):
        first = (rows // 2 + 15) // 16 * 16
        return (at, first) if sign > 0 else (at + first, rows - first)

    def z_ring(tag, rows_of, pys, first_deps, count):
        ids = {}
        for d in (1, 2, 3, 4):
            for s in (1, -1):
                src = 3 + s * (d - 1)
                dst = 3 + s * d if d < 4 else 7
                rows = rows_of(None) if d < 4 else rows_of(s)
                deps = [ids[d - 1, s]] if d > 1 else list(first_deps)
                ids[d, s] = add((tag, d, s), "z", s, (pys, (src, 1)), (pys, (dst, 1)), rows, deps, count * rows[-1] * 512)
        return ids

    def at_pz(ids, pz):
        dz = pz - 3
        if dz == 0:
            return []
        return [ids[4, 1], ids[4, -1]] if dz == 4 else [ids[abs(dz), 1 if dz > 0 else -1]]

    def y_ring(tag, rows_of, pz, deps, count):
        ids = {}
        for t in (1, -1):
            rows = rows_of(None)
            ids[1, t] = add((tag, 1, t), "y", t, ((1, 1), pz), ((1 + t, 1), pz), rows, list(deps), count * rows[-1] * 512)
        for t in (1, -1):
            rows = rows_of(t)
            ids[2, t] = add((tag, 2, t), "y", t, ((1 + t, 1), pz), ((3, 1), pz), rows, [ids[1, t]], count * rows[-1] * 512)
        return ids

    def x_rows(dx, sign):
        return ("x", dx) + ((0, Q) if sign is None else half(sign, 0, Q))

    def fixed(at, rows):
        return lambda sign: ("r",) + ((at, rows) if sign is None else half(sign, at, rows))

    xz = z_ring("xz", lambda s: x_rows(0, s), (1, 1), [], 1)
    zz = z_ring("zz", fixed(Z_AT, Z_ROWS), (1, 1), [], 1)
    yy = y_ring("yy", fixed(Y_AT, Y_ROWS), (3, 1), [], 1)
    xy = y_ring("xy", lambda s: x_rows(0, s), (0, 8), list(xz.values()), 8)
    x_groups = [
        (1, (2, 3), [xz[1, 1], xz[1, -1]]),
        (1, (0, 2), [xz[2, -1], xz[3, -1]]),
        (1, (5, 3), [xz[2, 1], xz[3, 1], xz[4, 1], xz[4, -1]]),
        (2, (0, 8), [xy[1, 1]]), (0, (0, 8), [xy[1, -1]]), (3, (0, 8), [xy[2, 1], xy[2, -1]])]
    for py, pz, deps in x_groups:
        place = ((py, 1), pz)
        first = {}
        for u in (1, -1):
            rows = x_rows(0, None)
            first[u] = add(("xx", py, pz, 1, u), "x", u, place, place, rows, list(deps), pz[1] * Q * 512)
        for u in (1, -1):
            rows = x_rows(u, u)
            add(("xx", py, pz, 2, u), "x", u, place, place, rows, [first[u]], pz[1] * rows[-1] * 512)
    for pz in (3, 4, 2, 5, 1, 6, 0, 7):
        y_ring(("zy", pz), fixed(Z_AT, Z_ROWS), (pz, 1), at_pz(zz, pz), 1)
    z_ring("yzA", fixed(Y_AT, Y_ROWS), (0, 2), [yy[1, -1]], 2)
    z_ring("yzB", fixed(Y_AT, Y_ROWS), (2, 2), [yy[1, 1], yy[2, 1], yy[2, -1]], 2)
    late = {("zz", 2): [xz[2, 1], xz[2, -1]], ("zz", 3): [xz[3, 1], xz[3, -1]], ("yzA", 1): [xz[4, 1], xz[4, -1]],
            ("yzB", 1): [xz[4, 1], xz[4, -1]]}
    for m in msgs:
        m["deps"] += late.get(m["name"][:2], [])
        if m["name"][0] in (("zy", 5), ("zy", 1)) and m["name"][1] == 1:
            m["deps"] += list(xz.values())
    for i, other in HOLD:
        msgs[i]["deps"].append(other)
    return msgs


def order(msgs, rate=45e3, latency=1.5):
    free = {}
    got = set()
    started = set()
    heap = []
    t_end = {}

    def issue(now):
        for i in RANK:
            m = msgs[i]
            if i not in started and all(d in got for d in m["deps"]):
                started.add(i)
                link = (m["dim"], m["sign"])
                begin = max(now, free.get(link, 0.0))
                free[link] = begin + m["bytes"] / rate
                heapq.heappush(heap, (free[link] + latency, i))

    issue(0.0)
    seq = []
    while heap:
        t, i = heapq.heappop(heap)
        got.add(i)
        seq.append(i)
        t_end[i] = t
        issue(t)
    return seq, t_end, free


def sweep(m_ref, k, nb=NB, group=GROUP):
    n = m_ref.shape[0]
    at = k * nb
    tiles = n // LANES
    home, off = at // LANES, at % LANES
    r = m_ref[at:at + nb, :]
    panel = [m_ref[at:at + nb, t * LANES:(t + 1) * LANES] for t in range(tiles)]
    lane = lax.broadcasted_iota(jnp.int32, (nb, LANES), 1)
    row = lax.broadcasted_iota(jnp.int32, (nb, LANES), 0)

    def spread(v):
        return jnp.broadcast_to(v, (nb, LANES))

    for j0 in range(0, nb, group):
        cols = [spread(panel[home][:, off + j:off + j + 1]) for j in range(j0, j0 + group)]
        rows = [[p[j:j + 1, :] for p in panel] for j in range(j0, j0 + group)]
        for i in range(group):
            j = j0 + i
            inv = 1.0 / cols[i][j:j + 1, :]
            here = lane[:1] == off + j
            scaled = [rows[i][t] * inv for t in range(tiles)]
            scaled[home] = jnp.where(here, inv, scaled[home])
            for a in range(i + 1, group):
                f = cols[a][j:j + 1, :] * inv
                cols[a] = jnp.where(row == j, spread(f), cols[a] - cols[i] * f)
                g = cols[i][j0 + a:j0 + a + 1, :]
                cleared = [rows[a][t] if t != home else jnp.where(here, 0.0, rows[a][t]) for t in range(tiles)]
                rows[a] = [cleared[t] - g * scaled[t] for t in range(tiles)]
            for t in range(tiles):
                old = panel[t] if t != home else jnp.where(lane == off + j, 0.0, panel[t])
                panel[t] = jnp.where(row == j, spread(scaled[t]), old - cols[i] * scaled[t])
    inside = (lane >= off) & (lane < off + nb)
    w = [jnp.where(inside, -p, p) if t == home else p for t, p in enumerate(panel)]
    upd = lax.dot_general(r, jnp.concatenate(w, axis=1), (((0,), (0,)), ((), ())), precision=HI,
                          preferred_element_type=jnp.float32)
    big = lax.broadcasted_iota(jnp.int32, (1, n), 1)
    m_ref[...] = jnp.where((big >= at) & (big < at + nb), 0.0, m_ref[...]) - upd
    for t in range(tiles):
        m_ref[at:at + nb, t * LANES:(t + 1) * LANES] = w[t]


def kernel(msgs, seq, unroll, coords, b_hbm, c_hbm, v_hbm, out, both, g, gsib, m, v, sums, away, pair, near, parts,
           own_sem, send, recv, sib_send, sib_recv, gs, gr, v_sem, s1, r1, s2, r2):
    grp, wide = lax.axis_index("grp"), lax.axis_index("wide")
    x, core = grp // 2, grp % 2
    y, z = wide // 8, wide % 8
    sib = (grp + 1 - 2 * core, wide)
    count = v_hbm.shape[0]
    mine = both.at[core]

    def dev(dim, s):
        if dim == "x":
            return (((x + s + 4) % 4) * 2 + core, wide)
        if dim == "y":
            return (grp, ((y + s + 4) % 4) * 8 + z)
        return (grp, y * 8 + (z + s + 8) % 8)

    def row_slice(rows):
        if rows[0] == "r":
            return pl.ds(rows[1] // G, rows[2] // G)
        return pl.ds(((x - rows[1] + 4) % 4) * (Q // G) + rows[2] // G, rows[3] // G)

    def region(place, rows):
        (py, npy), (pz, npz) = place
        return mine.at[pl.ds(py, npy), pl.ds(pz, npz), row_slice(rows)]

    peers = [dev(d, s) for d in "xyz" for s in (1, -1)] + [dev("x", 2), sib]
    bar = pltpu.get_barrier_semaphore()
    for p in peers:
        pl.semaphore_signal(bar, inc=1, device_id=p, device_id_type=MESH)

    own_rows = [("x", 0, 0, Q), ("r", Z_AT, SHARD - Z_AT)]
    own_place = ((1, 1), (3, 1))
    for k, src in enumerate((b_hbm, c_hbm)):
        @pl.when(core == k)
        def _():
            for j, rows in enumerate(own_rows):
                pltpu.make_async_copy(src.at[row_slice(rows)], mine.at[1, 3, row_slice(rows)], own_sem.at[j]).start()
    for j, rows in enumerate(own_rows):
        pltpu.make_async_copy(b_hbm.at[row_slice(rows)], mine.at[1, 3, row_slice(rows)], own_sem.at[j]).wait()
    pl.semaphore_wait(bar, len(peers))

    def copy(i):
        q = msgs[i]
        return pltpu.make_async_remote_copy(
            src_ref=region(q["src"], q["rows"]), dst_ref=region(q["dst"], q["rows"]),
            send_sem=send.at[i], recv_sem=recv.at[i], device_id=dev(q["dim"], q["sign"]), device_id_type=MESH)

    def hand_over(place, rows):
        pltpu.make_async_remote_copy(
            src_ref=region(place, rows), dst_ref=region(place, rows),
            send_sem=sib_send, recv_sem=sib_recv, device_id=sib, device_id_type=MESH).start()

    def add_gram(place, rows):
        (py, npy), (pz, npz) = place
        f = both[core, pl.ds(py, npy), pl.ds(pz, npz), row_slice(rows)].reshape(-1, R)
        g[...] += lax.dot_general(f, f, (((0,), (0,)), ((), ())), preferred_element_type=jnp.float32)

    started, got = set(), set()

    def issue():
        for i in RANK:
            if i not in started and all(d in got for d in msgs[i]["deps"]):
                started.add(i)
                copy(i).start()

    def value_copy(n):
        return pltpu.make_async_copy(v_hbm.at[n], v.at[n], v_sem.at[n])

    issue()
    for rows in own_rows:
        hand_over(own_place, rows)

    g[...] = jnp.zeros_like(g)
    for rows in own_rows:
        add_gram(own_place, rows)
    for k, i in enumerate(seq):
        copy(i).wait_recv()
        got.add(i)
        issue()
        if k >= 16 and k % 3 == 1 and (k - 16) // 3 < count:
            value_copy((k - 16) // 3).start()
        hand_over(msgs[i]["dst"], msgs[i]["landed"])
        add_gram(msgs[i]["dst"], msgs[i]["landed"])
    swap = pltpu.make_async_remote_copy(src_ref=g, dst_ref=gsib, send_sem=gs, recv_sem=gr, device_id=sib, device_id_type=MESH)
    swap.start()
    for i in range(len(msgs)):
        copy(i).wait_send()
    theirs = pltpu.make_async_remote_copy(src_ref=mine, dst_ref=both.at[1 - core], send_sem=sib_send, recv_sem=sib_recv,
                                          device_id=sib, device_id_type=MESH)
    theirs.wait()

    chunk = 512
    per = chunk // BS

    def factor_rows(k, n):
        at = coords[k + 1, n]
        py, pz, first = (y - (at >> 6) + 5) & 3, (z - (at >> 3) + 11) & 7, (at & 7) * (BS // G)
        return jnp.concatenate([both[k, py, pz, first + i] for i in range(BS // G)], axis=0)

    @pl.loop(0, count // unroll)
    def _(step):
        for u in range(unroll):
            value_copy(step * unroll + u).wait()
        for u in range(unroll):
            n = step * unroll + u
            b = factor_rows(0, n)
            c = factor_rows(1, n).astype(jnp.float32)
            for q in range(BS // per):
                prod = lax.dot_general(v[n, :, q * chunk:(q + 1) * chunk], b, (((0,), (0,)), ((), ())),
                                       preferred_element_type=jnp.float32)
                sums[n, q * per:(q + 1) * per, :] = jnp.sum(prod.reshape(per, BS, R) * c[None], axis=1)

    def owned_by(to_core, to_x, half):
        row = (to_x * 2 + to_core) * 2 + half
        total = jnp.zeros((BS, R), jnp.float32)
        for n in range(count):
            at = coords[0, n]
            miss = jnp.abs((at >> 6) * 2 + (at & 1) - row)
            total = total + sums[n] * (1 - jnp.minimum(miss, 1)).astype(jnp.float32)
        return total

    for to_x in range(4):
        for half in range(2):
            away[to_x, half * BS:(half + 1) * BS, :] = owned_by(1 - core, to_x, half)
    pass_on = pltpu.make_async_remote_copy(src_ref=away, dst_ref=pair, send_sem=s1, recv_sem=r1, device_id=sib,
                                           device_id_type=MESH)
    pass_on.start()
    for to_x in range(4):
        for half in range(2):
            near[to_x, half * BS:(half + 1) * BS, :] = owned_by(core, to_x, half)
    swap.wait()
    m[...] = g[...] * gsib[...]
    sweep(m, 0)
    pass_on.wait()
    near[...] += pair[...]
    far = []
    for d in (2, 1, 3):
        far.append(pltpu.make_async_remote_copy(
            src_ref=near.at[(x + d) % 4], dst_ref=parts.at[d - 1], send_sem=s2.at[d - 1], recv_sem=r2.at[d - 1],
            device_id=dev("x", d), device_id_type=MESH))
        far[-1].start()
    for k in range(1, R // NB):
        sweep(m, k)
    for q in far:
        q.wait()
    rows = near[x] + parts[0] + parts[1] + parts[2]
    out[...] = -jnp.dot(rows, m[...], precision=HI, preferred_element_type=jnp.float32)


def local(block_coords, block_values, factor_b, factor_c):
    msgs = plan()
    seq = order(msgs)[0]
    n = len(msgs)
    count = block_values.shape[0]
    rows = 2 * BS
    hbm = pl.BlockSpec(memory_space=pltpu.HBM)
    dma = pltpu.SemaphoreType.DMA
    square = pltpu.VMEM((R, R), jnp.float32)
    four = pltpu.VMEM((4, rows, R), jnp.float32)
    return pl.pallas_call(
        functools.partial(kernel, msgs, seq, 3),
        out_shape=jax.ShapeDtypeStruct((rows, R), jnp.float32),
        in_specs=[pl.BlockSpec(memory_space=pltpu.SMEM), hbm, hbm, hbm],
        out_specs=pl.BlockSpec(memory_space=pltpu.VMEM),
        scratch_shapes=[
            pltpu.VMEM((2, 4, 8, SHARD // G, G, R), jnp.bfloat16), square, square, square,
            pltpu.VMEM(block_values.shape, jnp.bfloat16), pltpu.VMEM((count, BS, R), jnp.float32), four, four, four,
            pltpu.VMEM((3, rows, R), jnp.float32),
            dma((2,)), dma((n,)), dma((n,)), dma, dma, dma, dma, dma((count,)), dma, dma, dma((3,)), dma((3,))],
        compiler_params=pltpu.CompilerParams(collective_id=0, has_side_effects=True, vmem_limit_bytes=56 << 20),
        name="als_update",
    )(block_coords.T, factor_b.reshape(-1, G, R), factor_c.reshape(-1, G, R), block_values)


def solution(mesh):
    in_specs = (P(("grp", "wide"), None), P(("grp", "wide"), None, None), P("wide", None), P("wide", None))
    return jax.shard_map(local, mesh=mesh, in_specs=in_specs, out_specs=P(("grp", "wide"), None), check_vma=False)
```

```python
import functools
import heapq

import jax
import jax.numpy as jnp
from jax import lax
from jax.experimental import pallas as pl
from jax.experimental.pallas import tpu as pltpu
from jax.sharding import PartitionSpec as P

MESH = pl.DeviceIdType.MESH
HI = lax.Precision.HIGHEST
BS, R = 64, 256
NB, GROUP, LANES = 64, 8, 128
SHARD, G = 512, 16
Q = 48
Z_AT, Z_ROWS = 4 * Q, 160
Y_AT, Y_ROWS = 4 * Q + 160, 160


RANK = (
    82, 6, 16, 93, 47, 53, 15, 18, 70, 80, 12, 75, 27, 21, 19, 30, 0, 33, 52, 83, 14, 5, 49, 50, 56, 35,
    94, 20, 39, 84, 81, 7, 25, 72, 88, 4, 40, 74, 71, 87, 29, 34, 59, 31, 32, 76, 62, 58, 43, 37, 57, 92,
    1, 85, 54, 26, 11, 60, 3, 17, 69, 28, 51, 61, 90, 67, 46, 24, 77, 65, 8, 23, 86, 63, 36, 64, 89, 38,
    22, 10, 68, 9, 55, 13, 44, 48, 79, 73, 78, 41, 2, 45, 66, 95, 42, 91)
HOLD = (
    (12, 52), (18, 17), (21, 13), (22, 61), (23, 5), (24, 17), (26, 58), (29, 9), (30, 6), (34, 49),
    (35, 16), (38, 64), (39, 10), (42, 24), (43, 38), (44, 68), (45, 56), (47, 3), (50, 22), (52, 49),
    (53, 17), (60, 51), (61, 49), (62, 72), (63, 52), (67, 22), (69, 73), (72, 30), (74, 12), (77, 10),
    (78, 60), (79, 0), (81, 59), (82, 26), (84, 56), (85, 53), (86, 23), (88, 29), (89, 3), (92, 83),
    (93, 60), (94, 64), (95, 81))


def plan():
    msgs = []

    def add(name, dim, sign, src, dst, rows, deps, nbytes):
        landed = ("x", rows[1] + sign) + rows[2:] if dim == "x" else rows
        msgs.append(dict(name=name, dim=dim, sign=sign, src=src, dst=dst, rows=rows, landed=landed, deps=deps, bytes=nbytes))
        return len(msgs) - 1

    def half(sign, at, rows):
        first = (rows // 2 + 15) // 16 * 16
        return (at, first) if sign > 0 else (at + first, rows - first)

    def z_ring(tag, rows_of, pys, first_deps, count):
        ids = {}
        for d in (1, 2, 3, 4):
            for s in (1, -1):
                src = 3 + s * (d - 1)
                dst = 3 + s * d if d < 4 else 7
                rows = rows_of(None) if d < 4 else rows_of(s)
                deps = [ids[d - 1, s]] if d > 1 else list(first_deps)
                ids[d, s] = add((tag, d, s), "z", s, (pys, (src, 1)), (pys, (dst, 1)), rows, deps, count * rows[-1] * 512)
        return ids

    def at_pz(ids, pz):
        dz = pz - 3
        if dz == 0:
            return []
        return [ids[4, 1], ids[4, -1]] if dz == 4 else [ids[abs(dz), 1 if dz > 0 else -1]]

    def y_ring(tag, rows_of, pz, deps, count):
        ids = {}
        for t in (1, -1):
            rows = rows_of(None)
            ids[1, t] = add((tag, 1, t), "y", t, ((1, 1), pz), ((1 + t, 1), pz), rows, list(deps), count * rows[-1] * 512)
        for t in (1, -1):
            rows = rows_of(t)
            ids[2, t] = add((tag, 2, t), "y", t, ((1 + t, 1), pz), ((3, 1), pz), rows, [ids[1, t]], count * rows[-1] * 512)
        return ids

    def x_rows(dx, sign):
        return ("x", dx) + ((0, Q) if sign is None else half(sign, 0, Q))

    def fixed(at, rows):
        return lambda sign: ("r",) + ((at, rows) if sign is None else half(sign, at, rows))

    xz = z_ring("xz", lambda s: x_rows(0, s), (1, 1), [], 1)
    zz = z_ring("zz", fixed(Z_AT, Z_ROWS), (1, 1), [], 1)
    yy = y_ring("yy", fixed(Y_AT, Y_ROWS), (3, 1), [], 1)
    xy = y_ring("xy", lambda s: x_rows(0, s), (0, 8), list(xz.values()), 8)
    x_groups = [
        (1, (2, 3), [xz[1, 1], xz[1, -1]]),
        (1, (0, 2), [xz[2, -1], xz[3, -1]]),
        (1, (5, 3), [xz[2, 1], xz[3, 1], xz[4, 1], xz[4, -1]]),
        (2, (0, 8), [xy[1, 1]]), (0, (0, 8), [xy[1, -1]]), (3, (0, 8), [xy[2, 1], xy[2, -1]])]
    for py, pz, deps in x_groups:
        place = ((py, 1), pz)
        first = {}
        for u in (1, -1):
            rows = x_rows(0, None)
            first[u] = add(("xx", py, pz, 1, u), "x", u, place, place, rows, list(deps), pz[1] * Q * 512)
        for u in (1, -1):
            rows = x_rows(u, u)
            add(("xx", py, pz, 2, u), "x", u, place, place, rows, [first[u]], pz[1] * rows[-1] * 512)
    for pz in (3, 4, 2, 5, 1, 6, 0, 7):
        y_ring(("zy", pz), fixed(Z_AT, Z_ROWS), (pz, 1), at_pz(zz, pz), 1)
    z_ring("yzA", fixed(Y_AT, Y_ROWS), (0, 2), [yy[1, -1]], 2)
    z_ring("yzB", fixed(Y_AT, Y_ROWS), (2, 2), [yy[1, 1], yy[2, 1], yy[2, -1]], 2)
    late = {("zz", 2): [xz[2, 1], xz[2, -1]], ("zz", 3): [xz[3, 1], xz[3, -1]], ("yzA", 1): [xz[4, 1], xz[4, -1]],
            ("yzB", 1): [xz[4, 1], xz[4, -1]]}
    for m in msgs:
        m["deps"] += late.get(m["name"][:2], [])
        if m["name"][0] in (("zy", 5), ("zy", 1)) and m["name"][1] == 1:
            m["deps"] += list(xz.values())
    for i, other in HOLD:
        msgs[i]["deps"].append(other)
    return msgs


def order(msgs, rate=45e3, latency=2.5):
    free = {}
    got = set()
    started = set()
    heap = []
    t_end = {}

    def issue(now):
        for i in RANK:
            m = msgs[i]
            if i not in started and all(d in got for d in m["deps"]):
                started.add(i)
                link = (m["dim"], m["sign"])
                begin = max(now, free.get(link, 0.0))
                free[link] = begin + m["bytes"] / rate
                heapq.heappush(heap, (free[link] + latency, i))

    issue(0.0)
    seq = []
    while heap:
        t, i = heapq.heappop(heap)
        got.add(i)
        seq.append(i)
        t_end[i] = t
        issue(t)
    return seq, t_end, free


def sweep(m_ref, k, nb=NB, group=GROUP):
    n = m_ref.shape[0]
    at = k * nb
    tiles = n // LANES
    home, off = at // LANES, at % LANES
    r = m_ref[at:at + nb, :]
    panel = [m_ref[at:at + nb, t * LANES:(t + 1) * LANES] for t in range(tiles)]
    lane = lax.broadcasted_iota(jnp.int32, (nb, LANES), 1)
    row = lax.broadcasted_iota(jnp.int32, (nb, LANES), 0)

    def spread(v):
        return jnp.broadcast_to(v, (nb, LANES))

    for j0 in range(0, nb, group):
        cols = [spread(panel[home][:, off + j:off + j + 1]) for j in range(j0, j0 + group)]
        rows = [[p[j:j + 1, :] for p in panel] for j in range(j0, j0 + group)]
        for i in range(group):
            j = j0 + i
            inv = 1.0 / cols[i][j:j + 1, :]
            here = lane[:1] == off + j
            scaled = [rows[i][t] * inv for t in range(tiles)]
            scaled[home] = jnp.where(here, inv, scaled[home])
            for a in range(i + 1, group):
                f = cols[a][j:j + 1, :] * inv
                cols[a] = jnp.where(row == j, spread(f), cols[a] - cols[i] * f)
                g = cols[i][j0 + a:j0 + a + 1, :]
                cleared = [rows[a][t] if t != home else jnp.where(here, 0.0, rows[a][t]) for t in range(tiles)]
                rows[a] = [cleared[t] - g * scaled[t] for t in range(tiles)]
            for t in range(tiles):
                old = panel[t] if t != home else jnp.where(lane == off + j, 0.0, panel[t])
                panel[t] = jnp.where(row == j, spread(scaled[t]), old - cols[i] * scaled[t])
    inside = (lane >= off) & (lane < off + nb)
    w = [jnp.where(inside, -p, p) if t == home else p for t, p in enumerate(panel)]
    upd = lax.dot_general(r, jnp.concatenate(w, axis=1), (((0,), (0,)), ((), ())), precision=HI,
                          preferred_element_type=jnp.float32)
    big = lax.broadcasted_iota(jnp.int32, (1, n), 1)
    m_ref[...] = jnp.where((big >= at) & (big < at + nb), 0.0, m_ref[...]) - upd
    for t in range(tiles):
        m_ref[at:at + nb, t * LANES:(t + 1) * LANES] = w[t]


def kernel(msgs, seq, unroll, coords, b_hbm, c_hbm, v_hbm, out, both, g, gsib, m, v, sums, away, pair, near, parts,
           own_sem, send, recv, sib_send, sib_recv, gs, gr, v_sem, s1, r1, s2, r2):
    grp, wide = lax.axis_index("grp"), lax.axis_index("wide")
    x, core = grp // 2, grp % 2
    y, z = wide // 8, wide % 8
    sib = (grp + 1 - 2 * core, wide)
    count = v_hbm.shape[0]
    mine = both.at[core]

    def dev(dim, s):
        if dim == "x":
            return (((x + s + 4) % 4) * 2 + core, wide)
        if dim == "y":
            return (grp, ((y + s + 4) % 4) * 8 + z)
        return (grp, y * 8 + (z + s + 8) % 8)

    def row_slice(rows):
        if rows[0] == "r":
            return pl.ds(rows[1] // G, rows[2] // G)
        return pl.ds(((x - rows[1] + 4) % 4) * (Q // G) + rows[2] // G, rows[3] // G)

    def region(place, rows):
        (py, npy), (pz, npz) = place
        return mine.at[pl.ds(py, npy), pl.ds(pz, npz), row_slice(rows)]

    peers = [dev(d, s) for d in "xyz" for s in (1, -1)] + [dev("x", 2), sib]
    bar = pltpu.get_barrier_semaphore()
    for p in peers:
        pl.semaphore_signal(bar, inc=1, device_id=p, device_id_type=MESH)

    own_rows = [("x", 0, 0, Q), ("r", Z_AT, SHARD - Z_AT)]
    own_place = ((1, 1), (3, 1))
    for k, src in enumerate((b_hbm, c_hbm)):
        @pl.when(core == k)
        def _():
            for j, rows in enumerate(own_rows):
                pltpu.make_async_copy(src.at[row_slice(rows)], mine.at[1, 3, row_slice(rows)], own_sem.at[j]).start()
    for j, rows in enumerate(own_rows):
        pltpu.make_async_copy(b_hbm.at[row_slice(rows)], mine.at[1, 3, row_slice(rows)], own_sem.at[j]).wait()
    pl.semaphore_wait(bar, len(peers))

    def copy(i):
        q = msgs[i]
        return pltpu.make_async_remote_copy(
            src_ref=region(q["src"], q["rows"]), dst_ref=region(q["dst"], q["rows"]),
            send_sem=send.at[i], recv_sem=recv.at[i], device_id=dev(q["dim"], q["sign"]), device_id_type=MESH)

    def hand_over(place, rows):
        pltpu.make_async_remote_copy(
            src_ref=region(place, rows), dst_ref=region(place, rows),
            send_sem=sib_send, recv_sem=sib_recv, device_id=sib, device_id_type=MESH).start()

    def add_gram(place, rows):
        (py, npy), (pz, npz) = place
        f = both[core, pl.ds(py, npy), pl.ds(pz, npz), row_slice(rows)].reshape(-1, R)
        g[...] += lax.dot_general(f, f, (((0,), (0,)), ((), ())), preferred_element_type=jnp.float32)

    started, got = set(), set()

    def issue():
        for i in RANK:
            if i not in started and all(d in got for d in msgs[i]["deps"]):
                started.add(i)
                copy(i).start()

    def value_copy(n):
        return pltpu.make_async_copy(v_hbm.at[n], v.at[n], v_sem.at[n])

    issue()
    for rows in own_rows:
        hand_over(own_place, rows)

    g[...] = jnp.zeros_like(g)
    for rows in own_rows:
        add_gram(own_place, rows)
    for k, i in enumerate(seq):
        copy(i).wait_recv()
        got.add(i)
        issue()
        if k >= 16 and k % 3 == 1 and (k - 16) // 3 < count:
            value_copy((k - 16) // 3).start()
        hand_over(msgs[i]["dst"], msgs[i]["landed"])
        add_gram(msgs[i]["dst"], msgs[i]["landed"])
    swap = pltpu.make_async_remote_copy(src_ref=g, dst_ref=gsib, send_sem=gs, recv_sem=gr, device_id=sib, device_id_type=MESH)
    swap.start()
    theirs = pltpu.make_async_remote_copy(src_ref=mine, dst_ref=both.at[1 - core], send_sem=sib_send, recv_sem=sib_recv,
                                          device_id=sib, device_id_type=MESH)
    theirs.wait()

    chunk = 512
    per = chunk // BS

    def factor_rows(k, n):
        at = coords[k + 1, n]
        py, pz, first = (y - (at >> 6) + 5) & 3, (z - (at >> 3) + 11) & 7, (at & 7) * (BS // G)
        return jnp.concatenate([both[k, py, pz, first + i] for i in range(BS // G)], axis=0)

    @pl.loop(0, count // unroll)
    def _(step):
        for u in range(unroll):
            value_copy(step * unroll + u).wait()
        for u in range(unroll):
            n = step * unroll + u
            b = factor_rows(0, n)
            c = factor_rows(1, n).astype(jnp.float32)
            for q in range(BS // per):
                prod = lax.dot_general(v[n, :, q * chunk:(q + 1) * chunk], b, (((0,), (0,)), ((), ())),
                                       preferred_element_type=jnp.float32)
                sums[n, q * per:(q + 1) * per, :] = jnp.sum(prod.reshape(per, BS, R) * c[None], axis=1)

    def owned_by(to_core, to_x, half):
        row = (to_x * 2 + to_core) * 2 + half
        total = jnp.zeros((BS, R), jnp.float32)
        for n in range(count):
            at = coords[0, n]
            miss = jnp.abs((at >> 6) * 2 + (at & 1) - row)
            total = total + sums[n] * (1 - jnp.minimum(miss, 1)).astype(jnp.float32)
        return total

    for to_x in range(4):
        for half in range(2):
            away[to_x, half * BS:(half + 1) * BS, :] = owned_by(1 - core, to_x, half)
    pass_on = pltpu.make_async_remote_copy(src_ref=away, dst_ref=pair, send_sem=s1, recv_sem=r1, device_id=sib,
                                           device_id_type=MESH)
    pass_on.start()
    for to_x in range(4):
        for half in range(2):
            near[to_x, half * BS:(half + 1) * BS, :] = owned_by(core, to_x, half)
    swap.wait()
    m[...] = g[...] * gsib[...]
    sweep(m, 0)
    pass_on.wait()
    near[...] += pair[...]
    far = []
    for d in (2, 1, 3):
        far.append(pltpu.make_async_remote_copy(
            src_ref=near.at[(x + d) % 4], dst_ref=parts.at[d - 1], send_sem=s2.at[d - 1], recv_sem=r2.at[d - 1],
            device_id=dev("x", d), device_id_type=MESH))
        far[-1].start()
    for k in range(1, R // NB):
        sweep(m, k)
    for q in far:
        q.wait()
    for i in range(len(msgs)):
        copy(i).wait_send()
    rows = near[x] + parts[0] + parts[1] + parts[2]
    out[...] = -jnp.dot(rows, m[...], precision=HI, preferred_element_type=jnp.float32)


def local(block_coords, block_values, factor_b, factor_c):
    msgs = plan()
    seq = order(msgs)[0]
    n = len(msgs)
    count = block_values.shape[0]
    rows = 2 * BS
    hbm = pl.BlockSpec(memory_space=pltpu.HBM)
    dma = pltpu.SemaphoreType.DMA
    square = pltpu.VMEM((R, R), jnp.float32)
    four = pltpu.VMEM((4, rows, R), jnp.float32)
    return pl.pallas_call(
        functools.partial(kernel, msgs, seq, 4),
        out_shape=jax.ShapeDtypeStruct((rows, R), jnp.float32),
        in_specs=[pl.BlockSpec(memory_space=pltpu.SMEM), hbm, hbm, hbm],
        out_specs=pl.BlockSpec(memory_space=pltpu.VMEM),
        scratch_shapes=[
            pltpu.VMEM((2, 4, 8, SHARD // G, G, R), jnp.bfloat16), square, square, square,
            pltpu.VMEM(block_values.shape, jnp.bfloat16), pltpu.VMEM((count, BS, R), jnp.float32), four, four, four,
            pltpu.VMEM((3, rows, R), jnp.float32),
            dma((2,)), dma((n,)), dma((n,)), dma, dma, dma, dma, dma((count,)), dma, dma, dma((3,)), dma((3,))],
        compiler_params=pltpu.CompilerParams(collective_id=0, has_side_effects=True, vmem_limit_bytes=56 << 20),
        name="als_update",
    )(block_coords.T, factor_b.reshape(-1, G, R), factor_c.reshape(-1, G, R), block_values)


def solution(mesh):
    in_specs = (P(("grp", "wide"), None), P(("grp", "wide"), None, None), P("wide", None), P("wide", None))
    return jax.shard_map(local, mesh=mesh, in_specs=in_specs, out_specs=P(("grp", "wide"), None), check_vma=False)
```
